32 devices in a mesh: rep: 8 (over z, core), shard: 4 (over y, x).
Axes of the slice: x: 2, y: 2, z: 4, core: 2. Of those that a mesh axis runs over, the one named last changes fastest.
Arguments:
- tokens: bfloat16 [8, 1024, 1536], P('rep', 'shard'), may hold values from -6 to 6
- cotangent: bfloat16 [8, 1024, 1536], P('rep', 'shard'), may hold values from -6 to 6
- segment_ids: int32 [8, 1024], P('rep'), may hold values from 0 to 15, never falling along the last dimension, each value on 1 to 512 neighbouring positions
- adapter_ids: int32 [8], P('rep'), may hold values from 0 to 7
- norm1_gain: float32 [1536], replicated, may hold values from 0.5 to 1.5
- query_key_value_weight: bfloat16 [1536, 3072], P('shard'), may hold values from -0.15625 to 0.15625
- w_attn_out: bfloat16 [1536, 1536], P('shard'), may hold values from -1.5 to 1.5
- norm2_gain: float32 [1536], replicated, may hold values from 0.5 to 1.5
- w_gate_up: bfloat16 [1536, 8192], P('shard'), may hold values from -0.15625 to 0.15625
- w_down: bfloat16 [4096, 1536], P('shard'), may hold values from -0.09375 to 0.09375
- adapter_a: bfloat16 [8, 212992], P(None, 'shard'), may hold values from -0.15625 to 0.15625
- adapter_b: bfloat16 [8, 229376], P(None, 'shard'), may hold values from -1.5 to 1.5
Outputs:
- output: bfloat16 [8, 1024, 1536], P('rep', 'shard')
- grad_tokens: float32 [8, 1024, 1536], P('rep', 'shard')
- grad_a: float32 [8, 212992], P(None, 'shard')
- grad_b: float32 [8, 229376], P(None, 'shard')
The draws below stay inside these ranges and needn't reach their ends.
Inputs may be any that keep to these rules, and one draw needn't show every extreme that they name: `segment_ids`: along each sequence the ids never fall, and each of the 16 ids appears in every sequence.
All inputs are finite; a program needn't handle non-finite values.
Results may differ from the reference program's by a relative error of at most 0.022.
Values may be sent and summed in bfloat16 or wider, within the bound.
No kernel may reach another device: no remote copies, remote signals or barrier semaphores. Data moves between devices by JAX's collectives and lax.ppermute only.
A program may use at most 192 MiB of HBM per device.

```python
import math
import jax
import jax.numpy as jnp
import numpy as np
from jax import lax

D = 1536
FF = 4096
HEADS = 16
KV_HEADS = 8
HEAD_DIM = 96
ADAPTER_RANK = 16
ADAPTERS = 8
DOCS = 16
LEN = 1024
SEQS = 8
A_SIZE = 212992
B_SIZE = 229376


def place_ends(values, own_key, least, largest):
    index_at = [jax.random.randint(jax.random.fold_in(own_key, axis), (), 0, length) for axis, length in enumerate(values.shape)]
    longest = values.shape.index(max(values.shape))
    next_to = index_at[:longest] + [(index_at[longest] + 1) % values.shape[longest]] + index_at[longest + 1:]
    return values.at[tuple(index_at)].set(least).at[tuple(next_to)].set(largest)


def levels(key, shape, shards, smallest, largest):
    def one(position, shards_of):
        steps = jax.random.uniform(jax.random.fold_in(jax.random.fold_in(key, 6), position), (shards_of,), jnp.float32, smallest / len(shards), largest / len(shards))
        return jnp.repeat(jnp.exp(steps), shape[position] // shards_of).reshape((-1,) + (1,) * (len(shape) - position - 1))

    factor_of = one(*shards[0])
    for cut in shards[1:]:
        factor_of = factor_of * one(*cut)
    return factor_of


def length_profile(amount, total, reach, skew):
    portions = [(1 << 20) // math.isqrt(rank ** skew) + 1 for rank in range(2, amount + 1)]
    rest, holding = total - reach - (amount - 1), [1] * (amount - 1)
    while rest > 0:
        movable = [i for i in range(amount - 1) if holding[i] < reach]
        pool, budget = sum([portions[i] for i in movable]), rest
        for i in movable:
            more = min(reach - holding[i], max(1, budget * portions[i] // pool), rest)
            holding[i] = holding[i] + more
            rest = rest - more
    return np.array([reach] + holding)


def ragged_sizes(own_key, amount, total, bound, skew):
    if amount == 2:
        one = jax.random.randint(own_key, (), max(1, total - bound), min(bound, total - 1) + 1)
        return jnp.stack([one, total - one])
    sizes = jnp.asarray(length_profile(amount, total, bound, skew), jnp.int32)
    pairs = (amount - 1) // 2
    source_of, sink = sizes[1:1 + 2 * pairs:2], sizes[2:2 + 2 * pairs:2]
    room = jnp.minimum(source_of - 1, bound - sink)
    moved = jax.random.randint(jax.random.fold_in(own_key, 1), (pairs,), 0, 1 << 20) % (room + 1)
    sizes = sizes.at[1:1 + 2 * pairs:2].set(source_of - moved).at[2:2 + 2 * pairs:2].set(sink + moved)
    return sizes[jax.random.permutation(jax.random.fold_in(own_key, 2), amount)]


def normal_values(stream_key, shape, scale, most, split=(), kind=jnp.bfloat16):
    entries = jax.random.normal(stream_key, shape, jnp.float32) * scale
    if len(split) > 0:
        entries = levels(stream_key, shape, split, -0.22, 0.18) * entries
    return jnp.clip(entries, min=-most, max=most).astype(kind)


def setup_inputs(seed: int = 0) -> dict:
    arg_keys = jax.random.split(jax.random.key(seed), 13)
    return {
        "tokens": normal_values(arg_keys[0], (SEQS, LEN, D), 1.0, 6.0, ((0, 8), (1, 4))),
        "cotangent": normal_values(arg_keys[1], (SEQS, LEN, D), 1.0, 6.0, ((0, 8), (1, 4))),
        "segment_ids": jax.vmap(lambda own: jnp.searchsorted(jnp.cumsum(ragged_sizes(own, DOCS, LEN, LEN // 2, 2)), jnp.arange(LEN), side="right"))(jax.random.split(arg_keys[2], SEQS)).reshape((SEQS, LEN)).astype(jnp.int32),
        "adapter_ids": place_ends(jax.random.randint(arg_keys[3], (SEQS,), 0, ADAPTERS), jax.random.fold_in(arg_keys[3], 1), 0, ADAPTERS - 1).astype(jnp.int32),
        "norm1_gain": jnp.clip(1.0 + 0.1 * jax.random.normal(arg_keys[4], (D,), jnp.float32), 0.5, 1.5),
        "query_key_value_weight": normal_values(arg_keys[5], (D, D + 2 * KV_HEADS * HEAD_DIM), D ** -0.5, 0.15625, ((0, 4),)),
        "w_attn_out": normal_values(arg_keys[6], (D, D), HEADS ** -0.5, 1.5, ((0, 4),)),
        "norm2_gain": jnp.clip(1.0 + 0.1 * jax.random.normal(arg_keys[7], (D,), jnp.float32), 0.5, 1.5),
        "w_gate_up": normal_values(arg_keys[8], (D, 2 * FF), D ** -0.5, 0.15625, ((0, 4),)),
        "w_down": normal_values(arg_keys[9], (FF, D), FF ** -0.5, 0.09375, ((0, 4),)),
        "adapter_a": normal_values(arg_keys[10], (ADAPTERS, A_SIZE), D ** -0.5, 0.15625, ((1, 4),)),
        "adapter_b": normal_values(arg_keys[11], (ADAPTERS, B_SIZE), ADAPTER_RANK ** -0.5, 1.5, ((1, 4),)),
    }


EPS = 1e-05
ROPE_BASE = 100000.0

@jax.custom_vjp
def low(v):
    return lax.optimization_barrier(v.astype(jnp.bfloat16)).astype(jnp.float32)

@jax.custom_vjp
def reduced_backward(v):
    return v

def low_keep(v):
    return (low(v), None)

def low_pass(kept, grad):
    return (grad,)

def back_keep(v):
    return (v, None)

def back_low(kept, grad):
    return (low(grad),)
low.defvjp(low_keep, low_pass)
reduced_backward.defvjp(back_keep, back_low)

def matrix_product(left, right):
    return jnp.dot(left, right, precision=lax.Precision.HIGHEST)

def enter_shapes():
    return [(3 * ADAPTER_RANK, D), (ADAPTER_RANK, D), (2 * ADAPTER_RANK, D), (ADAPTER_RANK, FF)]

def leave_shapes():
    kv_width = KV_HEADS * HEAD_DIM
    return [(ADAPTER_RANK, D), (ADAPTER_RANK, kv_width), (ADAPTER_RANK, kv_width), (ADAPTER_RANK, D), (ADAPTER_RANK, FF), (ADAPTER_RANK, FF), (ADAPTER_RANK, D)]

def unpack(flat, shapes):
    leading = flat.shape[:-1]
    result = []
    offset = 0
    for matrix_shape in shapes:
        extent = matrix_shape[0] * matrix_shape[1]
        result.append(flat[..., offset:offset + extent].reshape(leading + matrix_shape))
        offset = offset + extent
    return result

def rotary(positions):
    half_dim = HEAD_DIM // 2
    frequency = ROPE_BASE ** (-(jnp.arange(half_dim, dtype=jnp.float32) * 2.0 / HEAD_DIM))
    angles = positions.astype(jnp.float32)[:, None] * frequency[None, :]
    return (jnp.cos(angles), jnp.sin(angles))

def rotate(value_rows, cosine, sine_table):
    half_dim = value_rows.shape[-1] // 2
    former = value_rows[..., :half_dim]
    latter = value_rows[..., half_dim:]
    return jnp.concatenate([former * cosine - latter * sine_table, latter * cosine + former * sine_table], axis=-1)

def rms_norm(value_rows, norm_gain):
    return value_rows * lax.rsqrt(lax.optimization_barrier(jnp.mean(value_rows * value_rows, axis=-1, keepdims=True)) + EPS) * norm_gain

def layer(input_rows, flat_a, flat_b, segments, frozen):
    norm1_gain, query_key_value_weight, w_attn_out, norm2_gain, w_gate_up, w_down = frozen
    query_key_value_entry, output_entry, gate_up_entry, feedforward_entry = unpack(flat_a, enter_shapes())
    query_exit, key_exit, value_exit, output_exit, gate_exit, up_exit, feedforward_exit = unpack(flat_b, leave_shapes())
    length = input_rows.shape[0]
    kv_width = KV_HEADS * HEAD_DIM
    groups = HEADS // KV_HEADS
    first_normed = low(rms_norm(input_rows, norm1_gain))
    query_key_value_middle = reduced_backward(low(matrix_product(first_normed, query_key_value_entry.T)))
    adapter_query_key_value = jnp.concatenate([matrix_product(query_key_value_middle[:, :ADAPTER_RANK], query_exit), matrix_product(query_key_value_middle[:, ADAPTER_RANK:2 * ADAPTER_RANK], key_exit), matrix_product(query_key_value_middle[:, 2 * ADAPTER_RANK:], value_exit)], axis=-1)
    stacked_query_key_value = reduced_backward(matrix_product(first_normed, query_key_value_weight) + adapter_query_key_value)
    cosine, sine_table = rotary(jnp.arange(length, dtype=jnp.int32))
    cosine = cosine[:, None, :]
    sine_table = sine_table[:, None, :]
    queries = low(rotate(stacked_query_key_value[:, :D].reshape(length, HEADS, HEAD_DIM), cosine, sine_table))
    queries = queries.reshape(length, KV_HEADS, groups, HEAD_DIM)
    keys_rot = low(rotate(stacked_query_key_value[:, D:D + kv_width].reshape(length, KV_HEADS, HEAD_DIM), cosine, sine_table))
    values_low = low(stacked_query_key_value[:, D + kv_width:].reshape(length, KV_HEADS, HEAD_DIM))
    block_rows = min(512, length)
    key_pos = jnp.arange(length, dtype=jnp.int32)

    def attend(operands):
        query_block, begin_at = operands
        query_pos = begin_at + jnp.arange(block_rows, dtype=jnp.int32)
        query_seg = lax.dynamic_slice_in_dim(segments, begin_at, block_rows)
        allowed = jnp.logical_and(key_pos[None, :] <= query_pos[:, None], segments[None, :] == query_seg[:, None])
        scores = reduced_backward(jnp.einsum('tkgd,nkd->kgtn', query_block, keys_rot, precision=lax.Precision.HIGHEST) * HEAD_DIM ** (-0.5))
        unnormed = jnp.where(allowed, jnp.exp(scores), 0.0)
        totals = lax.optimization_barrier(jnp.sum(unnormed, axis=-1))
        weighted = reduced_backward(jnp.einsum('kgtn,nkd->tkgd', low(unnormed), values_low, precision=lax.Precision.HIGHEST))
        return weighted / jnp.transpose(totals, (2, 0, 1))[..., None]
    starts = jnp.arange(length // block_rows, dtype=jnp.int32) * block_rows
    query_blocks = queries.reshape(length // block_rows, block_rows, KV_HEADS, groups, HEAD_DIM)
    attended = lax.map(jax.checkpoint(attend), (query_blocks, starts)).reshape(length, D)
    attended_reduced = low(attended)
    output_middle = reduced_backward(low(matrix_product(attended_reduced, output_entry.T)))
    hidden_state = input_rows + reduced_backward(matrix_product(attended_reduced, w_attn_out) + matrix_product(output_middle, output_exit))
    second_normed = low(rms_norm(hidden_state, norm2_gain))
    gate_up_middle = reduced_backward(low(matrix_product(second_normed, gate_up_entry.T)))
    gate_up = reduced_backward(matrix_product(second_normed, w_gate_up) + jnp.concatenate([matrix_product(gate_up_middle[:, :ADAPTER_RANK], gate_exit), matrix_product(gate_up_middle[:, ADAPTER_RANK:], up_exit)], axis=-1))
    activated_rows = low(jax.nn.silu(gate_up[:, :FF]) * gate_up[:, FF:])
    feedforward_middle = reduced_backward(low(matrix_product(activated_rows, feedforward_entry.T)))
    return hidden_state + reduced_backward(matrix_product(activated_rows, w_down) + matrix_product(feedforward_middle, feedforward_exit))

def reference(tokens, cotangent, segment_ids, adapter_ids, norm1_gain, query_key_value_weight, w_attn_out, norm2_gain, w_gate_up, w_down, adapter_a, adapter_b):
    frozen = (norm1_gain.astype(jnp.float32), query_key_value_weight.astype(jnp.float32), w_attn_out.astype(jnp.float32), norm2_gain.astype(jnp.float32), w_gate_up.astype(jnp.float32), w_down.astype(jnp.float32))
    table_a = adapter_a.astype(jnp.float32)
    table_b = adapter_b.astype(jnp.float32)
    slots = jnp.arange(ADAPTERS, dtype=jnp.int32)

    def per_sequence(carry, operands):
        sum_a, sum_b = carry
        input_rows, upstream, segments, chosen = operands
        flat_a = table_a[chosen]
        flat_b = table_b[chosen]

        def closed(value_rows, first_a, first_b):
            return layer(value_rows, first_a, first_b, segments, frozen)
        outputs, pullback = jax.vjp(closed, input_rows.astype(jnp.float32), flat_a, flat_b)
        grad_inputs, grad_first_a, grad_first_b = pullback(upstream.astype(jnp.float32))
        marker = (slots == chosen).astype(jnp.float32)
        sum_a = sum_a + marker[:, None] * grad_first_a[None, :]
        sum_b = sum_b + marker[:, None] * grad_first_b[None, :]
        return ((sum_a, sum_b), (outputs.astype(jnp.bfloat16), grad_inputs))
    initial = (jnp.zeros((ADAPTERS, A_SIZE), jnp.float32), jnp.zeros((ADAPTERS, B_SIZE), jnp.float32))
    (sum_a, sum_b), (outputs, grad_tokens) = lax.scan(per_sequence, initial, (tokens, cotangent, segment_ids, adapter_ids))
    return (outputs, grad_tokens, sum_a, sum_b)
```

```python
import functools

import jax
import jax.numpy as jnp
import numpy as np
from jax import lax
from jax.experimental import pallas as pl
from jax.experimental.pallas import tpu as pltpu
from jax.sharding import PartitionSpec as P

D = 1536
FF = 4096
HEADS = 16
KV_HEADS = 8
HEAD_DIM = 96
RANK = 16
ADAPTERS = 8
EPS = 1e-05
ROPE_BASE = 100000.0
KVW = KV_HEADS * HEAD_DIM
QKV = D + 2 * KVW
HALF = HEAD_DIM // 2
SCALE = HEAD_DIM ** (-0.5)
TILE = 4 * HEAD_DIM
NEG = -1e30

F32 = jnp.float32
BF16 = jnp.bfloat16
ANY = pl.BlockSpec(memory_space=pl.ANY)
SMEM = pl.BlockSpec(memory_space=pltpu.SMEM)
VM = pl.BlockSpec(memory_space=pltpu.VMEM)


def dot(a, b):
    return lax.dot_general(a, b, (((1,), (0,)), ((), ())), preferred_element_type=F32)


def dnt(a, b):
    return lax.dot_general(a, b, (((1,), (1,)), ((), ())), preferred_element_type=F32)


def call(body, name, outs, ins, specs, scratch, flops, nbytes, vmem=60):
    return pl.pallas_call(
        body,
        name=name,
        out_shape=outs,
        in_specs=specs,
        out_specs=jax.tree.map(lambda _: VM, outs),
        scratch_shapes=scratch,
        compiler_params=pltpu.CompilerParams(vmem_limit_bytes=vmem << 20),
        cost_estimate=pl.CostEstimate(
            flops=int(flops), bytes_accessed=int(nbytes), transcendentals=0
        ),
    )(*ins)


def sds(shape, dtype):
    return jax.ShapeDtypeStruct(shape, dtype)


def rot_pairs(rows, cos, sin, heads, back):
    out = []
    for h in range(heads):
        u1 = rows[h * HEAD_DIM : h * HEAD_DIM + HALF]
        u2 = rows[h * HEAD_DIM + HALF : (h + 1) * HEAD_DIM]
        if back:
            out += [u1 * cos + u2 * sin, u2 * cos - u1 * sin]
        else:
            out += [u1 * cos - u2 * sin, u2 * cos + u1 * sin]
    return jnp.concatenate(out, axis=0)


def column_copies(pieces, arrs, offs, buf, sem, slot, col, width):
    return [
        pltpu.make_async_copy(
            arrs[a].at[pl.ds(src, n), pl.ds(col, width)],
            buf.at[slot, pl.ds(pl.multiple_of(offs[i], 16), n)],
            sem.at[slot, i],
        )
        for i, (a, src, n) in enumerate(pieces)
    ]


def qkv_body(pieces, na, offs, x_ref, g_ref, e_ref, l_ref, cos_ref, sin_ref, *rest):
    arrs = rest[:na]
    q_ref, kv_ref, n1_ref, m1t_ref, buf, m_ref, sem = rest[na:]
    nt = QKV // TILE

    def copies(j, slot):
        return column_copies(pieces, arrs, offs, buf, sem, slot, pl.multiple_of(j * TILE, 128), TILE)

    for j in range(2):
        for c in copies(j, j):
            c.start()
    x = x_ref[...].astype(F32)
    r = lax.rsqrt(jnp.mean(x * x, axis=-1, keepdims=True) + EPS)
    n1 = (x * r * g_ref[...]).astype(BF16)
    n1_ref[...] = n1
    for b in range(3):
        e = e_ref[b * RANK : (b + 1) * RANK]
        m_ref[b] = dnt(n1, e).astype(BF16)
        m1t_ref[b * RANK : (b + 1) * RANK] = dnt(e, n1).astype(BF16)

    def step(j, carry):
        slot = lax.rem(j, 2)
        for c in copies(j, slot):
            c.wait()
        isq = j < D // TILE
        isv = j >= (D + KVW) // TILE
        blk = jnp.where(isq, 0, jnp.where(isv, 2, 1))
        y = dot(n1_ref[...], buf[slot]) + dot(
            m_ref[blk], l_ref[:, pl.ds(pl.multiple_of(j * TILE, 128), TILE)]
        )

        @pl.when(j + 2 < nt)
        def _():
            for c in copies(j + 2, slot):
                c.start()

        yt = y.T
        cos = jnp.where(isv, 1.0, cos_ref[...])
        sin = jnp.where(isv, 0.0, sin_ref[...])
        out = rot_pairs(yt, cos, sin, TILE // HEAD_DIM, False).astype(BF16)

        @pl.when(isq)
        def _():
            q_ref[pl.ds(pl.multiple_of(j * TILE, 128), TILE)] = out

        @pl.when(jnp.logical_not(isq))
        def _():
            kv_ref[pl.ds(pl.multiple_of(j * TILE - D, 128), TILE)] = out

        return carry

    lax.fori_loop(0, nt, step, 0)


def qkv_forward(pieces, offs, x, gain, e, lcat, cos, sin, arrs):
    rows = x.shape[0]
    return call(
        functools.partial(qkv_body, pieces, len(arrs)),
        "qkv_fwd",
        (
            sds((D, rows), BF16),
            sds((2 * KVW, rows), BF16),
            sds((rows, D), BF16),
            sds((3 * RANK, rows), BF16),
        ),
        [offs, x, gain, e, lcat, cos, sin, *arrs],
        [SMEM] + [VM] * 6 + [ANY] * len(arrs),
        [
            pltpu.VMEM((2, D, TILE), BF16),
            pltpu.VMEM((3, rows, RANK), BF16),
            pltpu.SemaphoreType.DMA((2, len(pieces))),
        ],
        2 * rows * D * QKV,
        2 * D * QKV,
    )


def fill_mask(mask_ref, base, qseg, kseg_ref, rows, blocks):
    qpos = base + lax.broadcasted_iota(jnp.int32, (rows, rows), 1)
    for b in range(blocks):
        kpos = base - b * rows + lax.broadcasted_iota(jnp.int32, (rows, rows), 0)
        same = kseg_ref[b * rows : (b + 1) * rows] == qseg
        ok = jnp.logical_and(jnp.logical_and(kpos <= qpos, kpos >= 0), same)
        one = jnp.where(ok, 1.0, 0.0)
        mask_ref[b] = jnp.concatenate([one, one], axis=1)


def turned(block):
    pad = jnp.zeros((128 - HEAD_DIM, block.shape[1]), F32)
    return jnp.concatenate([block.astype(F32), pad], axis=0).T.astype(BF16)


def padded(block):
    pad = jnp.zeros((128 - HEAD_DIM, block.shape[1]), F32)
    return jnp.concatenate([block.astype(F32), pad], axis=0).astype(BF16)


def attn_body(blocks, base_ref, qseg_ref, kseg_ref, q_ref, *rest):
    kvs = rest[:blocks]
    ot_ref, l_ref, o_ref, mask_ref = rest[blocks:]
    rows = q_ref.shape[1]
    fill_mask(mask_ref, base_ref[0], qseg_ref[...], kseg_ref, rows, blocks)

    def head(c, carry):
        at = pl.multiple_of(c * 2 * HEAD_DIM, 32)
        ka = pl.multiple_of(c * HEAD_DIM, 32)
        q2 = jnp.concatenate(
            [q_ref[pl.ds(at, HEAD_DIM)], q_ref[pl.ds(at + HEAD_DIM, HEAD_DIM)]], axis=1
        )
        q2p = padded(q2)
        total = jnp.zeros((1, 2 * rows), F32)
        w = jnp.zeros((HEAD_DIM, 2 * rows), F32)
        for b in range(blocks):
            k = turned(kvs[b][pl.ds(ka, HEAD_DIM)])
            v = kvs[b][pl.ds(KVW + ka, HEAD_DIM)]
            s = dot(k, q2p) * SCALE
            e = jnp.exp(jnp.where(mask_ref[b] > 0.5, s, NEG))
            total = total + jnp.sum(e, axis=0, keepdims=True)
            w = w + dot(v, e.astype(BF16))
        o = w / total
        ot_ref[pl.ds(at, HEAD_DIM)] = o[:, :rows]
        ot_ref[pl.ds(at + HEAD_DIM, HEAD_DIM)] = o[:, rows:]
        l_ref[c] = total
        return carry

    lax.fori_loop(0, KV_HEADS, head, 0)

    def turn(j, carry):
        at = pl.multiple_of(j * TILE, 128)
        o_ref[:, pl.ds(at, TILE)] = ot_ref[pl.ds(at, TILE)].T.astype(BF16)
        return carry

    lax.fori_loop(0, D // TILE, turn, 0)


def attention_forward(base, qseg, kseg, q, kvs):
    rows = q.shape[1]
    blocks = len(kvs)
    return call(
        functools.partial(attn_body, blocks),
        "attn_fwd",
        (
            sds((D, rows), F32),
            sds((KV_HEADS, 1, 2 * rows), F32),
            sds((rows, D), BF16),
        ),
        [base, qseg, kseg, q, *kvs],
        [SMEM] + [VM] * (3 + blocks),
        [pltpu.VMEM((blocks, rows, 2 * rows), F32)],
        4 * rows * rows * blocks * D,
        2 * rows * D * 4,
    )


def attn_back_body(blocks, base_ref, qseg_ref, kseg_ref, q_ref, gw_ref, dl_ref, *rest):
    kvs = rest[:blocks]
    gq_ref = rest[blocks]
    gkv = rest[blocks + 1 : 2 * blocks + 1]
    mask_ref = rest[2 * blocks + 1]
    rows = q_ref.shape[1]
    fill_mask(mask_ref, base_ref[0], qseg_ref[...], kseg_ref, rows, blocks)

    def head(c, carry):
        at = pl.multiple_of(c * 2 * HEAD_DIM, 32)
        ka = pl.multiple_of(c * HEAD_DIM, 32)
        q2 = jnp.concatenate(
            [q_ref[pl.ds(at, HEAD_DIM)], q_ref[pl.ds(at + HEAD_DIM, HEAD_DIM)]], axis=1
        )
        gw2 = jnp.concatenate(
            [gw_ref[pl.ds(at, HEAD_DIM)], gw_ref[pl.ds(at + HEAD_DIM, HEAD_DIM)]], axis=1
        )
        q2p = padded(q2)
        gw2p = padded(gw2)
        delta = dl_ref[c]
        gq = jnp.zeros((HEAD_DIM, 2 * rows), F32)
        for b in range(blocks):
            kt = kvs[b][pl.ds(ka, HEAD_DIM)]
            vt = kvs[b][pl.ds(KVW + ka, HEAD_DIM)]
            s = dot(turned(kt), q2p) * SCALE
            e = jnp.exp(jnp.where(mask_ref[b] > 0.5, s, NEG))
            gp = dot(turned(vt), gw2p)
            ds = (e * (gp - delta)).astype(BF16)
            gq = gq + dot(kt, ds)
            gk = dnt(q2, ds) * SCALE
            gv = dnt(gw2, e.astype(BF16))
            gkv[b][pl.ds(ka, HEAD_DIM)] = gk.astype(gkv[b].dtype)
            gkv[b][pl.ds(KVW + ka, HEAD_DIM)] = gv.astype(gkv[b].dtype)
        gq = gq * SCALE
        gq_ref[pl.ds(at, HEAD_DIM)] = gq[:, :rows]
        gq_ref[pl.ds(at + HEAD_DIM, HEAD_DIM)] = gq[:, rows:]
        return carry

    lax.fori_loop(0, KV_HEADS, head, 0)


def attention_backward(base, qseg, kseg, q, gw, delta, kvs):
    rows = q.shape[1]
    blocks = len(kvs)
    return call(
        functools.partial(attn_back_body, blocks),
        "attn_bwd",
        (
            sds((D, rows), F32),
            sds((2 * KVW, rows), F32),
            *[sds((2 * KVW, rows), BF16) for _ in range(blocks - 1)],
        ),
        [base, qseg, kseg, q, gw, delta, *kvs],
        [SMEM] + [VM] * (5 + blocks),
        [pltpu.VMEM((blocks, rows, 2 * rows), F32)],
        10 * rows * rows * blocks * D,
        2 * rows * D * 8,
    )


def out_body(pieces, na, offs, o_ref, x_ref, g_ref, e_ref, l_ref, *rest):
    arrs = rest[:na]
    h_ref, n2_ref, mt_ref, buf, sem = rest[na:]
    nt = D // TILE

    def copies(j, slot):
        return column_copies(pieces, arrs, offs, buf, sem, slot, pl.multiple_of(j * TILE, 128), TILE)

    for j in range(2):
        for c in copies(j, j):
            c.start()
    m = dnt(o_ref[...], e_ref[...]).astype(BF16)
    mt_ref[...] = dnt(e_ref[...], o_ref[...]).astype(BF16)

    def step(j, carry):
        slot = lax.rem(j, 2)
        at = pl.multiple_of(j * TILE, 128)
        for c in copies(j, slot):
            c.wait()
        y = dot(o_ref[...], buf[slot]) + dot(m, l_ref[:, pl.ds(at, TILE)])

        @pl.when(j + 2 < nt)
        def _():
            for c in copies(j + 2, slot):
                c.start()

        h_ref[:, pl.ds(at, TILE)] = x_ref[:, pl.ds(at, TILE)].astype(F32) + y
        return carry

    lax.fori_loop(0, nt, step, 0)
    h = h_ref[...]
    r = lax.rsqrt(jnp.mean(h * h, axis=-1, keepdims=True) + EPS)
    n2_ref[...] = (h * r * g_ref[...]).astype(BF16)


def out_forward(pieces, offs, o_low, x, gain, e, lo, arrs):
    rows = x.shape[0]
    return call(
        functools.partial(out_body, pieces, len(arrs)),
        "out_fwd",
        (sds((rows, D), F32), sds((rows, D), BF16), sds((RANK, rows), BF16)),
        [offs, o_low, x, gain, e, lo, *arrs],
        [SMEM] + [VM] * 5 + [ANY] * len(arrs),
        [pltpu.VMEM((2, D, TILE), BF16), pltpu.SemaphoreType.DMA((2, len(pieces)))],
        2 * rows * D * D,
        2 * D * D,
    )


def wide(rows16):
    pad = jnp.zeros((128 - rows16.shape[0], rows16.shape[1]), F32)
    return jnp.concatenate([rows16, pad], axis=0).T.astype(BF16)


def mlp_body(pieces, tiles, na, nd, tf, half, *refs):
    offs, pos, n2_ref, ct_ref, e_ref, ed_ref, lg_ref, lu_ref, ld_ref = refs[:9]
    arrs = refs[9 : 9 + na]
    downs = refs[9 + na : 9 + na + nd]
    rest = refs[9 + na + nd :]
    own_ref, oth_ref, gown_ref, goth_ref, dlg_ref, dlu_ref, ded_ref, dld_ref, deg_ref = rest[:9]
    wg, wu, wd, acc, gacc, mg, mu, mgt, mut, gm, gmt, tacc, sem, dsem = rest[9:]
    rows = own_ref.shape[0]
    nt = len(tiles)

    def col(j):
        return pl.multiple_of(pos[j] * tf, 128)

    def copies(j, slot):
        at = col(j)
        return column_copies(pieces, arrs, offs, wg, sem.at[0], slot, at, tf) + column_copies(
            pieces, arrs, offs, wu, sem.at[1], slot, pl.multiple_of(half + at, 128), tf
        )

    def down_copy(j, slot):
        a, src = tiles[j]
        return pltpu.make_async_copy(downs[a].at[pl.ds(src, tf)], wd.at[slot], dsem.at[slot])

    def start(j, slot):
        for c in copies(j, slot):
            c.start()
        for jj in range(nt):

            @pl.when(j == jj)
            def _(jj=jj):
                down_copy(jj, slot).start()

    start(0, 0)
    start(1, 1)
    n2 = n2_ref[...]
    ct = ct_ref[...]
    eg = e_ref[:RANK]
    eu = e_ref[RANK:]
    mg[...] = dnt(n2, eg).astype(BF16)
    mu[...] = dnt(n2, eu).astype(BF16)
    mgt[...] = dnt(eg, n2).astype(BF16)
    mut[...] = dnt(eu, n2).astype(BF16)
    gm[...] = dnt(ct, ld_ref[...]).astype(BF16)
    gmt[...] = dnt(ld_ref[...], ct).astype(BF16)
    acc[...] = jnp.zeros_like(acc)
    gacc[...] = jnp.zeros_like(gacc)
    tacc[...] = jnp.zeros_like(tacc)

    def step(j, carry):
        slot = lax.rem(j, 2)
        at = col(j)
        for c in copies(j, slot):
            c.wait()
        down_copy(0, slot).wait()
        cols = pl.ds(at, tf)
        lg = lg_ref[:, cols]
        lu = lu_ref[:, cols]
        ed = ed_ref[:, cols]
        gate = dot(n2_ref[...], wg[slot]) + dot(mg[...], lg)
        up = dot(n2_ref[...], wu[slot]) + dot(mu[...], lu)
        gact = dnt(ct_ref[...], wd[slot]) + dot(gm[...], ed)
        sig = 1.0 / (1.0 + jnp.exp(-gate))
        silu = gate * sig
        act = (silu * up).astype(BF16)
        ggate = (gact * up * sig * (1.0 + gate * (1.0 - sig))).astype(BF16)
        gup = (gact * silu).astype(BF16)
        acc[...] += dot(act, wd[slot])
        gacc[...] += dnt(ggate, wg[slot]) + dnt(gup, wu[slot])
        tacc[0] += dnt(ed, act)
        tacc[1] += dnt(lg, ggate)
        tacc[2] += dnt(lu, gup)
        dlg_ref[:, cols] = dot(mgt[...], ggate)
        dlu_ref[:, cols] = dot(mut[...], gup)
        ded_ref[:, cols] = dot(gmt[...], act)

        @pl.when(j + 2 < nt)
        def _():
            start(j + 2, slot)

        return carry

    lax.fori_loop(0, nt, step, 0)
    zrow = jnp.zeros((128 - RANK, D), BF16)
    md = tacc[0]
    acc[...] += dot(wide(md), jnp.concatenate([ld_ref[...], zrow], axis=0))
    dld_ref[...] = dot(md.astype(BF16), ct_ref[...])
    for i in range(2):
        g = tacc[1 + i]
        e = e_ref[i * RANK : (i + 1) * RANK]
        gacc[...] += dot(wide(g), jnp.concatenate([e, zrow], axis=0))
        deg_ref[i * RANK : (i + 1) * RANK] = dot(g.astype(BF16), n2_ref[...])
    own_ref[...] = acc[:rows]
    oth_ref[...] = acc[rows:].astype(BF16)
    gown_ref[...] = gacc[:rows]
    goth_ref[...] = gacc[rows:].astype(BF16)


def mlp(pieces, tiles, tf, half, offs, pos, n2, ct, e, ed, lg, lu, ld, arrs, downs):
    m = n2.shape[0]
    rows = m // 2
    return call(
        functools.partial(mlp_body, pieces, tiles, len(arrs), len(downs), tf, half),
        "mlp",
        (
            sds((rows, D), F32),
            sds((rows, D), BF16),
            sds((rows, D), F32),
            sds((rows, D), BF16),
            sds((RANK, half), F32),
            sds((RANK, half), F32),
            sds((RANK, half), F32),
            sds((RANK, D), F32),
            sds((2 * RANK, D), F32),
        ),
        [offs, pos, n2, ct, e, ed, lg, lu, ld, *arrs, *downs],
        [SMEM, SMEM] + [VM] * 7 + [ANY] * (len(arrs) + len(downs)),
        [
            pltpu.VMEM((2, D, tf), BF16),
            pltpu.VMEM((2, D, tf), BF16),
            pltpu.VMEM((2, tf, D), BF16),
            pltpu.VMEM((m, D), F32),
            pltpu.VMEM((m, D), F32),
            pltpu.VMEM((m, RANK), BF16),
            pltpu.VMEM((m, RANK), BF16),
            pltpu.VMEM((RANK, m), BF16),
            pltpu.VMEM((RANK, m), BF16),
            pltpu.VMEM((m, RANK), BF16),
            pltpu.VMEM((RANK, m), BF16),
            pltpu.VMEM((3, RANK, m), F32),
            pltpu.SemaphoreType.DMA((2, 2, len(pieces))),
            pltpu.SemaphoreType.DMA((2,)),
        ],
        12 * m * D * half,
        6 * D * half,
    )


def out_back_body(pieces, na, *refs):
    offs, gn_ref, gx_ref, ct_ref, h_ref, g_ref, o_ref, ot_ref, l_ref, mt_ref, lo_ref, et_ref = refs[:12]
    arrs = refs[12 : 12 + na]
    gh_ref, gw_ref, dl_ref, dlo_ref, deo_ref, buf, sem = refs[12 + na :]
    rows = h_ref.shape[0]
    copies = [
        pltpu.make_async_copy(
            arrs[a].at[pl.ds(src, n)], buf.at[pl.ds(pl.multiple_of(offs[i], 16), n)], sem.at[i]
        )
        for i, (a, src, n) in enumerate(pieces)
    ]
    for c in copies:
        c.start()
    h = h_ref[...]
    r = lax.rsqrt(jnp.mean(h * h, axis=-1, keepdims=True) + EPS)
    sc = (gn_ref[...] + gx_ref[...].astype(F32)) * g_ref[...]
    gh = ct_ref[...].astype(F32) + r * sc - h * (r * r * r) * jnp.mean(sc * h, axis=-1, keepdims=True)
    gh_ref[...] = gh
    gb = gh.astype(BF16)
    gmt = dnt(lo_ref[...], gb).astype(BF16)
    dlo_ref[...] = dot(mt_ref[...], gb)
    deo_ref[...] = dot(gmt, o_ref[...])
    for c in copies:
        c.wait()

    def pair(c, carry):
        at = pl.multiple_of(c * 2 * HEAD_DIM, 64)
        g = dnt(buf[pl.ds(at, 2 * HEAD_DIM)], gb) + dot(et_ref[pl.ds(at, 2 * HEAD_DIM)], gmt)
        ot = ot_ref[pl.ds(at, 2 * HEAD_DIM)]
        for i in range(2):
            gi = g[i * HEAD_DIM : (i + 1) * HEAD_DIM]
            inv = 1.0 / l_ref[c][:, i * rows : (i + 1) * rows]
            gw_ref[pl.ds(at + i * HEAD_DIM, HEAD_DIM)] = (gi * inv).astype(BF16)
            d = jnp.sum(gi * ot[i * HEAD_DIM : (i + 1) * HEAD_DIM], axis=0, keepdims=True) * inv
            dl_ref[c, :, i * rows : (i + 1) * rows] = d
        return carry

    lax.fori_loop(0, KV_HEADS, pair, 0)


def out_backward(pieces, offs, gn, gx, ct, h, gain, o_low, ot, ls, mt, lo, et, arrs):
    rows = h.shape[0]
    return call(
        functools.partial(out_back_body, pieces, len(arrs)),
        "out_bwd",
        (
            sds((rows, D), F32),
            sds((D, rows), BF16),
            sds((KV_HEADS, 1, 2 * rows), F32),
            sds((RANK, D), F32),
            sds((RANK, D), F32),
        ),
        [offs, gn, gx, ct, h, gain, o_low, ot, ls, mt, lo, et, *arrs],
        [SMEM] + [VM] * 11 + [ANY] * len(arrs),
        [pltpu.VMEM((D, D), BF16), pltpu.SemaphoreType.DMA((len(pieces),))],
        2 * rows * D * D,
        2 * D * D,
    )


def qkv_back_body(pieces, na, nx, *refs):
    offs, gq_ref, gkv_ref = refs[:3]
    rxs = refs[3 : 3 + nx]
    cos_ref, sin_ref, m1t_ref, n1_ref, x_ref, g_ref, gh_ref, l_ref, et_ref = refs[3 + nx : 12 + nx]
    arrs = refs[12 + nx : 12 + nx + na]
    gt_ref, dl_ref, de_ref, buf, acc, gm, sem = refs[12 + nx + na :]
    nt = QKV // TILE

    def copies(j, slot):
        return column_copies(pieces, arrs, offs, buf, sem, slot, pl.multiple_of(j * TILE, 128), TILE)

    for j in range(2):
        for c in copies(j, j):
            c.start()
    acc[...] = jnp.zeros_like(acc)
    gm[...] = jnp.zeros_like(gm)

    def step(j, carry):
        slot = lax.rem(j, 2)
        isq = j < D // TILE
        isv = j >= (D + KVW) // TILE
        blk = jnp.where(isq, 0, jnp.where(isv, 2, 1))
        at = pl.multiple_of(j * TILE, 128)
        kv_at = pl.multiple_of(jnp.maximum(at - D, 0), 128)
        gkv = gkv_ref[pl.ds(kv_at, TILE)]
        for rx in rxs:
            gkv = gkv + rx[pl.ds(kv_at, TILE)].astype(F32)
        q_at = pl.multiple_of(jnp.minimum(at, D - TILE), 128)
        g = jnp.where(isq, gq_ref[pl.ds(q_at, TILE)], gkv)
        cos = jnp.where(isv, 1.0, cos_ref[...])
        sin = jnp.where(isv, 0.0, sin_ref[...])
        g = rot_pairs(g, cos, sin, TILE // HEAD_DIM, True).astype(BF16)
        row = pl.ds(pl.multiple_of(blk * RANK, 16), RANK)
        dl_ref[:, pl.ds(at, TILE)] = dnt(m1t_ref[row], g)
        gm[row] += dot(l_ref[:, pl.ds(at, TILE)], g)
        for c in copies(j, slot):
            c.wait()
        acc[...] += dot(buf[slot], g)

        @pl.when(j + 2 < nt)
        def _():
            for c in copies(j + 2, slot):
                c.start()

        return carry

    lax.fori_loop(0, nt, step, 0)
    gmb = gm[...].astype(BF16)
    de_ref[...] = dot(gmb, n1_ref[...])
    acc[...] += dot(et_ref[...], gmb)
    x = x_ref[...].astype(F32)
    r = lax.rsqrt(jnp.mean(x * x, axis=-1, keepdims=True) + EPS)
    sc = acc[...].T * g_ref[...]
    gt_ref[...] = gh_ref[...] + r * sc - x * (r * r * r) * jnp.mean(sc * x, axis=-1, keepdims=True)


def qkv_backward(pieces, offs, gq, gkv, rxs, cos, sin, m1t, n1, x, gain, gh, lcat, et, arrs):
    rows = x.shape[0]
    return call(
        functools.partial(qkv_back_body, pieces, len(arrs), len(rxs)),
        "qkv_bwd",
        (sds((rows, D), F32), sds((RANK, QKV), F32), sds((3 * RANK, D), F32)),
        [offs, gq, gkv, *rxs, cos, sin, m1t, n1, x, gain, gh, lcat, et, *arrs],
        [SMEM] + [VM] * (11 + len(rxs)) + [ANY] * len(arrs),
        [
            pltpu.VMEM((2, D, TILE), BF16),
            pltpu.VMEM((D, rows), F32),
            pltpu.VMEM((3 * RANK, rows), F32),
            pltpu.SemaphoreType.DMA((2, len(pieces))),
        ],
        2 * rows * D * QKV,
        2 * D * QKV,
    )


def split_flat(flat, shapes):
    out = []
    at = 0
    for a, b in shapes:
        out.append(flat[at : at + a * b].reshape(a, b))
        at += a * b
    return out


A_SHAPES = [(3 * RANK, D), (RANK, D), (2 * RANK, D), (RANK, FF)]
B_SHAPES = [(RANK, D), (RANK, KVW), (RANK, KVW), (RANK, D), (RANK, FF), (RANK, FF), (RANK, D)]


def shards(ns, nr, tokens, cotangent, segment_ids, adapter_ids, gain1, w_qkv, w_out, gain2, w_gu, w_down, table_a, table_b):
    assert tokens.shape[0] == 1
    x = tokens[0]
    ct = cotangent[0]
    seg = segment_ids[0]
    rows = x.shape[0]
    length = seg.shape[0]
    s = lax.axis_index("shard")
    r = lax.axis_index("rep")
    group = ns // 2
    h = s // group
    half = FF // 2

    def over(v, k):
        return lax.ppermute(v, "shard", [(i, i ^ k) for i in range(ns)])

    def swap(v, k):
        return lax.ppermute(v, "rep", [(i, i ^ k) for i in range(nr)])

    def shift(v, k):
        return lax.ppermute(v, "shard", [(i, i + k) for i in range(ns) if 0 <= i + k < ns])

    def gather(own, ks, send):
        n = own.shape[0]
        parts = 4 if n % 64 == 0 and nr % 4 == 0 else 1
        q = n // parts
        me = r & (parts - 1)
        cat = jnp.concatenate(
            [over(lax.dynamic_slice_in_dim(send(k), me * q, q, 0), k) for k in ks], axis=0
        )
        arrs = [own, cat]
        flips = [0]
        if parts == 4:
            far = swap(cat, 2)
            arrs += [far, swap(cat, 1), swap(far, 1)]
            flips = [0, 2, 1, 3]
        pieces = [(0, 0, n)]
        kv, fv = [0], [-1]
        for ai, f in enumerate(flips):
            for ki, k in enumerate(ks):
                pieces.append((1 + ai, ki * q, q))
                kv.append(k)
                fv.append(f)
        kv, fv = np.array(kv, np.int32), np.array(fv, np.int32)
        part = jnp.where(fv < 0, 0, me ^ jnp.maximum(fv, 0))
        return arrs, pieces, (s ^ kv), part, q

    every = list(range(1, ns))
    near = list(range(1, group))

    a = adapter_ids[0]
    row_a = lax.dynamic_slice_in_dim(table_a, a, 1, 0)[0]
    row_b = lax.dynamic_slice_in_dim(table_b, a, 1, 0)[0]
    na, nb = row_a.shape[0], row_b.shape[0]
    both = lax.all_gather(jnp.concatenate([row_a, row_b]), "shard", axis=0)
    e_qkv, e_out, e_gu, e_down = split_flat(both[:, :na].reshape(-1), A_SHAPES)
    l_q, l_k, l_v, l_out, l_gate, l_up, l_down = split_flat(both[:, na:].reshape(-1), B_SHAPES)
    lcat = jnp.concatenate([l_q, l_k, l_v], axis=1)

    qkv_arrs, qkv_pieces, sh, part, q = gather(w_qkv, every, lambda k: w_qkv)
    qkv_offs = (sh * w_qkv.shape[0] + part * q).astype(jnp.int32)
    out_arrs, out_pieces, sh, part, q = gather(w_out, every, lambda k: w_out)
    out_offs = (sh * w_out.shape[0] + part * q).astype(jnp.int32)
    gu4 = w_gu.reshape(w_gu.shape[0], 2, 2, half)

    def gu_half(i):
        return lax.dynamic_index_in_dim(gu4, i, 2, keepdims=False).reshape(w_gu.shape[0], 2 * half)

    gu_own, gu_other = gu_half(h), gu_half(1 - h)
    gu_arrs, gu_pieces, sh, part, q = gather(
        gu_own, every, lambda k: gu_own if k < group else gu_other
    )
    gu_offs = (sh * w_gu.shape[0] + part * q).astype(jnp.int32)
    down_arrs, down_pieces, sh, part, q = gather(w_down, near, lambda k: w_down)
    tf = 256
    tiles, base_of, add = [], [], []
    for i, (ai, src, n) in enumerate(down_pieces):
        for t in range(n // tf):
            tiles.append((ai, src + t * tf))
            base_of.append(i)
            add.append(t)
    start = ((sh % group) * w_down.shape[0] + part * q) // tf
    pos = (start[np.array(base_of)] + np.array(add, np.int32)).astype(jnp.int32)

    positions = s * rows + jnp.arange(rows, dtype=jnp.int32)
    freq = ROPE_BASE ** (-(jnp.arange(HALF, dtype=F32) * 2.0 / HEAD_DIM))
    angles = freq[:, None] * positions.astype(F32)[None, :]
    cos, sin = jnp.cos(angles), jnp.sin(angles)

    halo = min(ns - 1, -(-(length // 2 - 1) // rows))
    base = (s * rows).reshape(1).astype(jnp.int32)
    qseg = lax.dynamic_slice_in_dim(seg, s * rows, rows, 0)[None, :]
    kseg = jnp.concatenate(
        [
            lax.dynamic_slice_in_dim(seg, jnp.maximum(s - b, 0) * rows, rows, 0)
            for b in range(halo + 1)
        ]
    )[:, None]
    g1 = gain1[None, :]
    g2 = gain2[None, :]

    qt, kvt, n1, m1t = qkv_forward(qkv_pieces, qkv_offs, x, g1, e_qkv, lcat, cos, sin, qkv_arrs)
    kvs = [kvt] + [shift(kvt, b) for b in range(1, halo + 1)]
    ot, ls, o_low = attention_forward(base, qseg, kseg, qt, kvs)
    hidden, n2, mt = out_forward(out_pieces, out_offs, o_low, x, g2, e_out, l_out, out_arrs)
    n2_both = jnp.concatenate([n2, over(n2, group)], axis=0)
    ct_both = jnp.concatenate([ct, over(ct, group)], axis=0)

    def half_cols(v):
        return lax.dynamic_slice_in_dim(v, h * half, half, 1)

    own, oth, gown, goth, dlg, dlu, ded, dld, deg = mlp(
        gu_pieces,
        tiles,
        tf,
        half,
        gu_offs,
        pos,
        n2_both,
        ct_both,
        e_gu,
        half_cols(e_down),
        half_cols(l_gate),
        half_cols(l_up),
        l_down,
        gu_arrs,
        down_arrs,
    )
    gx = over(goth, group)
    output = (hidden + own + over(oth, group).astype(F32)).astype(BF16)
    gh, gw, delta, dlo, deo = out_backward(
        out_pieces, out_offs, gown, gx, ct, hidden, g2, o_low, ot, ls, mt, l_out, e_out.T, out_arrs
    )
    grads = attention_backward(base, qseg, kseg, qt, gw, delta, kvs)
    rxs = [shift(g, -b) for b, g in enumerate(grads[2:], 1)]
    grad_tokens, dlcat, deq = qkv_backward(
        qkv_pieces, qkv_offs, grads[0], grads[1], rxs, cos, sin, m1t, n1, x, g1, gh, lcat, e_qkv.T, qkv_arrs
    )

    def full_cols(v):
        return lax.dynamic_update_slice_in_dim(jnp.zeros((RANK, FF), BF16), v.astype(BF16), h * half, 1)

    def flat(parts, width):
        return jnp.concatenate([v.astype(BF16).reshape(-1) for v in parts]).reshape(ns, width)

    ga = flat([deq, deo, deg, full_cols(ded)], na)
    gb = flat(
        [dlcat[:, :D], dlcat[:, D : D + KVW], dlcat[:, D + KVW :], dlo, full_cols(dlg), full_cols(dlu), dld],
        nb,
    )
    mine = lax.all_to_all(jnp.concatenate([ga, gb], axis=1), "shard", 0, 0, tiled=True)
    mine = jnp.sum(mine.astype(F32), axis=0)
    hot = (adapter_ids[0] == jnp.arange(128)).astype(F32)
    line = jnp.concatenate([mine, hot]).astype(BF16)[None]
    k = 1
    while k < nr:
        line = jnp.concatenate([line, swap(line, k)], axis=0)
        k *= 2
    pick = line[:, na + nb : na + nb + ADAPTERS]
    total = lax.dot_general(
        pick, line[:, : na + nb], (((0,), (0,)), ((), ())), preferred_element_type=F32
    )
    return output[None], grad_tokens[None], total[:, :na], total[:, na:]


def solution(mesh):
    ns, nr = mesh.shape["shard"], mesh.shape["rep"]
    seqs = P("rep", "shard", None)
    frozen = P("shard", None)
    tables = P(None, "shard")
    return jax.shard_map(
        functools.partial(shards, ns, nr),
        mesh=mesh,
        in_specs=(seqs, seqs, P("rep", None), P("rep"), P(), frozen, frozen, P(), frozen, frozen, tables, tables),
        out_specs=(seqs, seqs, tables, tables),
        check_vma=False,
    )
```

```python
import functools

import jax
import jax.numpy as jnp
import numpy as np
from jax import lax
from jax.experimental import pallas as pl
from jax.experimental.pallas import tpu as pltpu
from jax.sharding import PartitionSpec as P

D = 1536
FF = 4096
HEADS = 16
KV_HEADS = 8
HEAD_DIM = 96
RANK = 16
ADAPTERS = 8
EPS = 1e-05
ROPE_BASE = 100000.0
KVW = KV_HEADS * HEAD_DIM
QKV = D + 2 * KVW
HALF = HEAD_DIM // 2
SCALE = HEAD_DIM ** (-0.5)
TILE = 4 * HEAD_DIM
NEG = -1e30

F32 = jnp.float32
BF16 = jnp.bfloat16
ANY = pl.BlockSpec(memory_space=pl.ANY)
SMEM = pl.BlockSpec(memory_space=pltpu.SMEM)
VM = pl.BlockSpec(memory_space=pltpu.VMEM)


def dot(a, b):
    return lax.dot_general(a, b, (((1,), (0,)), ((), ())), preferred_element_type=F32)


def dnt(a, b):
    return lax.dot_general(a, b, (((1,), (1,)), ((), ())), preferred_element_type=F32)


def call(body, name, outs, ins, specs, scratch, flops, nbytes, vmem=60):
    return pl.pallas_call(
        body,
        name=name,
        out_shape=outs,
        in_specs=specs,
        out_specs=jax.tree.map(lambda _: VM, outs),
        scratch_shapes=scratch,
        compiler_params=pltpu.CompilerParams(vmem_limit_bytes=vmem << 20),
        cost_estimate=pl.CostEstimate(
            flops=int(flops), bytes_accessed=int(nbytes), transcendentals=0
        ),
    )(*ins)


def sds(shape, dtype):
    return jax.ShapeDtypeStruct(shape, dtype)


def rot_pairs(rows, cos, sin, heads, back):
    out = []
    for h in range(heads):
        u1 = rows[h * HEAD_DIM : h * HEAD_DIM + HALF]
        u2 = rows[h * HEAD_DIM + HALF : (h + 1) * HEAD_DIM]
        if back:
            out += [u1 * cos + u2 * sin, u2 * cos - u1 * sin]
        else:
            out += [u1 * cos - u2 * sin, u2 * cos + u1 * sin]
    return jnp.concatenate(out, axis=0)


def column_copies(pieces, arrs, offs, buf, sem, slot, col, width):
    return [
        pltpu.make_async_copy(
            arrs[a].at[pl.ds(src, n), pl.ds(col, width)],
            buf.at[slot, pl.ds(pl.multiple_of(offs[i], 16), n)],
            sem.at[slot, i],
        )
        for i, (a, src, n) in enumerate(pieces)
    ]


def project_tiles(lo, hi, pieces, arrs, offs, n1_ref, m_ref, l_ref, cos_ref, sin_ref, out_ref, buf, sem):
    def copies(j, slot):
        return column_copies(pieces, arrs, offs, buf, sem, slot, pl.multiple_of(j * TILE, 128), TILE)

    def step(i, carry):
        j = lo + i
        slot = lax.rem(i, 2)
        for c in copies(j, slot):
            c.wait()
        isv = j >= (D + KVW) // TILE
        blk = jnp.where(j < D // TILE, 0, jnp.where(isv, 2, 1))
        y = dot(n1_ref[...], buf[slot]) + dot(
            m_ref[blk], l_ref[:, pl.ds(pl.multiple_of(j * TILE, 128), TILE)]
        )

        @pl.when(j + 2 < hi)
        def _():
            for c in copies(j + 2, slot):
                c.start()

        yt = y.T
        cos = jnp.where(isv, 1.0, cos_ref[...])
        sin = jnp.where(isv, 0.0, sin_ref[...])
        out = rot_pairs(yt, cos, sin, TILE // HEAD_DIM, False).astype(BF16)
        out_ref[pl.ds(pl.multiple_of(i * TILE, 128), TILE)] = out
        return carry

    return copies, lambda: lax.fori_loop(0, hi - lo, step, 0)


def kv_body(pieces, na, offs, x_ref, g_ref, e_ref, l_ref, cos_ref, sin_ref, *rest):
    arrs = rest[:na]
    kv_ref, n1_ref, m1t_ref, m_ref, buf, sem = rest[na:]
    lo, hi = D // TILE, QKV // TILE
    copies, run = project_tiles(
        lo, hi, pieces, arrs, offs, n1_ref, m_ref, l_ref, cos_ref, sin_ref, kv_ref, buf, sem
    )
    for j in range(2):
        for c in copies(lo + j, j):
            c.start()
    x = x_ref[...].astype(F32)
    r = lax.rsqrt(jnp.mean(x * x, axis=-1, keepdims=True) + EPS)
    n1 = (x * r * g_ref[...]).astype(BF16)
    n1_ref[...] = n1
    for b in range(3):
        e = e_ref[b * RANK : (b + 1) * RANK]
        m_ref[b] = dnt(n1, e).astype(BF16)
        m1t_ref[b * RANK : (b + 1) * RANK] = dnt(e, n1).astype(BF16)
    run()


def q_body(pieces, na, offs, n1_ref, m_ref, l_ref, cos_ref, sin_ref, *rest):
    arrs = rest[:na]
    q_ref, buf, sem = rest[na:]
    copies, run = project_tiles(
        0, D // TILE, pieces, arrs, offs, n1_ref, m_ref, l_ref, cos_ref, sin_ref, q_ref, buf, sem
    )
    for j in range(2):
        for c in copies(j, j):
            c.start()
    run()


def kv_forward(pieces, offs, x, gain, e, lcat, cos, sin, arrs):
    rows = x.shape[0]
    return call(
        functools.partial(kv_body, pieces, len(arrs)),
        "kv_fwd",
        (
            sds((2 * KVW, rows), BF16),
            sds((rows, D), BF16),
            sds((3 * RANK, rows), BF16),
            sds((3, rows, RANK), BF16),
        ),
        [offs, x, gain, e, lcat, cos, sin, *arrs],
        [SMEM] + [VM] * 6 + [ANY] * len(arrs),
        [pltpu.VMEM((2, D, TILE), BF16), pltpu.SemaphoreType.DMA((2, len(pieces)))],
        2 * rows * D * 2 * KVW,
        2 * D * 2 * KVW,
    )


def q_forward(pieces, offs, n1, m, lcat, cos, sin, arrs):
    rows = n1.shape[0]
    return call(
        functools.partial(q_body, pieces, len(arrs)),
        "q_fwd",
        sds((D, rows), BF16),
        [offs, n1, m, lcat, cos, sin, *arrs],
        [SMEM] + [VM] * 5 + [ANY] * len(arrs),
        [pltpu.VMEM((2, D, TILE), BF16), pltpu.SemaphoreType.DMA((2, len(pieces)))],
        2 * rows * D * D,
        2 * D * D,
    )


def fill_mask(mask_ref, base, qseg, kseg_ref, rows, numbers):
    qpos = base + lax.broadcasted_iota(jnp.int32, (rows, rows), 1)
    for i, b in enumerate(numbers):
        kpos = base - b * rows + lax.broadcasted_iota(jnp.int32, (rows, rows), 0)
        same = kseg_ref[i * rows : (i + 1) * rows] == qseg
        ok = jnp.logical_and(jnp.logical_and(kpos <= qpos, kpos >= 0), same)
        one = jnp.where(ok, 1.0, 0.0)
        mask_ref[i] = jnp.concatenate([one, one], axis=1)


def turned(block):
    pad = jnp.zeros((128 - HEAD_DIM, block.shape[1]), F32)
    return jnp.concatenate([block.astype(F32), pad], axis=0).T.astype(BF16)


def padded(block):
    pad = jnp.zeros((128 - HEAD_DIM, block.shape[1]), F32)
    return jnp.concatenate([block.astype(F32), pad], axis=0).astype(BF16)


def attn_body(blocks, base_ref, qseg_ref, kseg_ref, q_ref, *rest):
    kvs = rest[:blocks]
    ot_ref, l_ref, o_ref, mask_ref = rest[blocks:]
    rows = q_ref.shape[1]
    fill_mask(mask_ref, base_ref[0], qseg_ref[...], kseg_ref, rows, list(range(blocks)))

    def head(c, carry):
        at = pl.multiple_of(c * 2 * HEAD_DIM, 32)
        ka = pl.multiple_of(c * HEAD_DIM, 32)
        q2 = jnp.concatenate(
            [q_ref[pl.ds(at, HEAD_DIM)], q_ref[pl.ds(at + HEAD_DIM, HEAD_DIM)]], axis=1
        )
        q2p = padded(q2)
        total = jnp.zeros((1, 2 * rows), F32)
        w = jnp.zeros((HEAD_DIM, 2 * rows), F32)
        for b in range(blocks):
            k = turned(kvs[b][pl.ds(ka, HEAD_DIM)])
            v = kvs[b][pl.ds(KVW + ka, HEAD_DIM)]
            s = dot(k, q2p) * SCALE
            e = jnp.exp(jnp.where(mask_ref[b] > 0.5, s, NEG))
            total = total + jnp.sum(e, axis=0, keepdims=True)
            w = w + dot(v, e.astype(BF16))
        o = w / total
        ot_ref[pl.ds(at, HEAD_DIM)] = o[:, :rows]
        ot_ref[pl.ds(at + HEAD_DIM, HEAD_DIM)] = o[:, rows:]
        l_ref[c] = total
        return carry

    lax.fori_loop(0, KV_HEADS, head, 0)

    def turn(j, carry):
        at = pl.multiple_of(j * TILE, 128)
        o_ref[:, pl.ds(at, TILE)] = ot_ref[pl.ds(at, TILE)].T.astype(BF16)
        return carry

    lax.fori_loop(0, D // TILE, turn, 0)


def attention_forward(base, qseg, kseg, q, kvs):
    rows = q.shape[1]
    blocks = len(kvs)
    return call(
        functools.partial(attn_body, blocks),
        "attn_fwd",
        (
            sds((D, rows), F32),
            sds((KV_HEADS, 1, 2 * rows), F32),
            sds((rows, D), BF16),
        ),
        [base, qseg, kseg, q, *kvs],
        [SMEM] + [VM] * (3 + blocks),
        [pltpu.VMEM((blocks, rows, 2 * rows), F32)],
        4 * rows * rows * blocks * D,
        2 * rows * D * 4,
    )


def attn_back_body(numbers, first, base_ref, qseg_ref, kseg_ref, q_ref, gw_ref, dl_ref, *rest):
    blocks = len(numbers)
    kvs = rest[:blocks]
    rest = rest[blocks:]
    if not first:
        old_ref, rest = rest[0], rest[1:]
    gq_ref = rest[0]
    gkv = rest[1 : blocks + 1]
    mask_ref = rest[blocks + 1]
    rows = q_ref.shape[1]
    fill_mask(mask_ref, base_ref[0], qseg_ref[...], kseg_ref, rows, numbers)

    def head(c, carry):
        at = pl.multiple_of(c * 2 * HEAD_DIM, 32)
        ka = pl.multiple_of(c * HEAD_DIM, 32)
        lo, hi = pl.ds(at, HEAD_DIM), pl.ds(at + HEAD_DIM, HEAD_DIM)
        q2 = jnp.concatenate([q_ref[lo], q_ref[hi]], axis=1)
        gw2 = jnp.concatenate([gw_ref[lo], gw_ref[hi]], axis=1)
        q2p = padded(q2)
        gw2p = padded(gw2)
        delta = dl_ref[c]
        gq = jnp.zeros((HEAD_DIM, 2 * rows), F32)
        for b in range(blocks):
            kt = kvs[b][pl.ds(ka, HEAD_DIM)]
            vt = kvs[b][pl.ds(KVW + ka, HEAD_DIM)]
            s = dot(turned(kt), q2p) * SCALE
            e = jnp.exp(jnp.where(mask_ref[b] > 0.5, s, NEG))
            gp = dot(turned(vt), gw2p)
            ds = (e * (gp - delta)).astype(BF16)
            gq = gq + dot(kt, ds)
            gk = dnt(q2, ds) * SCALE
            gv = dnt(gw2, e.astype(BF16))
            gkv[b][pl.ds(ka, HEAD_DIM)] = gk.astype(gkv[b].dtype)
            gkv[b][pl.ds(KVW + ka, HEAD_DIM)] = gv.astype(gkv[b].dtype)
        gq = gq * SCALE
        if first:
            gq_ref[lo] = gq[:, :rows]
            gq_ref[hi] = gq[:, rows:]
        else:
            gq_ref[lo] = old_ref[lo] + gq[:, :rows]
            gq_ref[hi] = old_ref[hi] + gq[:, rows:]
        return carry

    lax.fori_loop(0, KV_HEADS, head, 0)


def attention_backward(numbers, base, qseg, kseg, q, gw, delta, kvs, old, dtype):
    rows = q.shape[1]
    blocks = len(kvs)
    first = old is None
    extra = [] if first else [old]
    return call(
        functools.partial(attn_back_body, numbers, first),
        "attn_bwd",
        (sds((D, rows), F32), *[sds((2 * KVW, rows), dtype) for _ in range(blocks)]),
        [base, qseg, kseg, q, gw, delta, *kvs, *extra],
        [SMEM] + [VM] * (5 + blocks + len(extra)),
        [pltpu.VMEM((blocks, rows, 2 * rows), F32)],
        10 * rows * rows * blocks * D,
        2 * rows * D * 8,
    )


def out_body(pieces, na, offs, o_ref, x_ref, g_ref, e_ref, l_ref, *rest):
    arrs = rest[:na]
    h_ref, n2_ref, mt_ref, buf, sem = rest[na:]
    nt = D // TILE

    def copies(j, slot):
        return column_copies(pieces, arrs, offs, buf, sem, slot, pl.multiple_of(j * TILE, 128), TILE)

    for j in range(2):
        for c in copies(j, j):
            c.start()
    m = dnt(o_ref[...], e_ref[...]).astype(BF16)
    mt_ref[...] = dnt(e_ref[...], o_ref[...]).astype(BF16)

    def step(j, carry):
        slot = lax.rem(j, 2)
        at = pl.multiple_of(j * TILE, 128)
        for c in copies(j, slot):
            c.wait()
        y = dot(o_ref[...], buf[slot]) + dot(m, l_ref[:, pl.ds(at, TILE)])

        @pl.when(j + 2 < nt)
        def _():
            for c in copies(j + 2, slot):
                c.start()

        h_ref[:, pl.ds(at, TILE)] = x_ref[:, pl.ds(at, TILE)].astype(F32) + y
        return carry

    lax.fori_loop(0, nt, step, 0)
    h = h_ref[...]
    r = lax.rsqrt(jnp.mean(h * h, axis=-1, keepdims=True) + EPS)
    n2_ref[...] = (h * r * g_ref[...]).astype(BF16)


def out_forward(pieces, offs, o_low, x, gain, e, lo, arrs):
    rows = x.shape[0]
    return call(
        functools.partial(out_body, pieces, len(arrs)),
        "out_fwd",
        (sds((rows, D), F32), sds((rows, D), BF16), sds((RANK, rows), BF16)),
        [offs, o_low, x, gain, e, lo, *arrs],
        [SMEM] + [VM] * 5 + [ANY] * len(arrs),
        [pltpu.VMEM((2, D, TILE), BF16), pltpu.SemaphoreType.DMA((2, len(pieces)))],
        2 * rows * D * D,
        2 * D * D,
    )


def wide(rows16):
    pad = jnp.zeros((128 - rows16.shape[0], rows16.shape[1]), F32)
    return jnp.concatenate([rows16, pad], axis=0).T.astype(BF16)


def mlp_body(pieces, tiles, na, nd, tf, width, first, last, *refs):
    offs, pos, base, n2_ref, ct_ref, e_ref, ed_ref, lg_ref, lu_ref, ld_ref = refs[:10]
    own_w = refs[10]
    arrs = refs[10 : 10 + na]
    downs = refs[10 + na : 10 + na + nd]
    refs = refs[10 + na + nd :]
    if not first:
        old, refs = refs[:3], refs[3:]
    if last:
        outs, refs = refs[:9], refs[9:]
        own_ref, oth_ref, gown_ref, goth_ref, dlg_ref, dlu_ref, ded_ref, dld_ref, deg_ref = outs
        acc, gacc, tacc, *refs = refs
        rows = own_ref.shape[0]
    else:
        acc, gacc, tacc, dlg_ref, dlu_ref, ded_ref, *refs = refs
    wg, wu, wd, mg, mu, mgt, mut, gm, gmt, sem, dsem = refs
    nt = len(tiles)

    def col(j):
        return pl.multiple_of(pos[j] * tf, 128)

    def copies(j, slot):
        at = col(j)
        out = []
        for i, (a, src, n) in enumerate(pieces):
            dst = pl.ds(pl.multiple_of(offs[i], 16), n)
            for g, w in enumerate((wg, wu)):
                if a == 0:
                    c = pl.multiple_of(base[0] + g * FF + at, 128)
                else:
                    c = pl.multiple_of(g * width + at, 128)
                out.append(
                    pltpu.make_async_copy(
                        arrs[a].at[pl.ds(src, n), pl.ds(c, tf)], w.at[slot, dst], sem.at[g, slot, i]
                    )
                )
        return out

    def down_copy(j, slot):
        a, src = tiles[j]
        return pltpu.make_async_copy(downs[a].at[pl.ds(src, tf)], wd.at[slot], dsem.at[slot])

    def start(j, slot):
        for c in copies(j, slot):
            c.start()
        for jj in range(nt):

            @pl.when(j == jj)
            def _(jj=jj):
                down_copy(jj, slot).start()

    start(0, 0)
    if nt > 1:
        start(1, 1)
    n2 = n2_ref[...]
    ct = ct_ref[...]
    eg = e_ref[:RANK]
    eu = e_ref[RANK:]
    mg[...] = dnt(n2, eg).astype(BF16)
    mu[...] = dnt(n2, eu).astype(BF16)
    mgt[...] = dnt(eg, n2).astype(BF16)
    mut[...] = dnt(eu, n2).astype(BF16)
    gm[...] = dnt(ct, ld_ref[...]).astype(BF16)
    gmt[...] = dnt(ld_ref[...], ct).astype(BF16)
    if first:
        acc[...] = jnp.zeros_like(acc)
        gacc[...] = jnp.zeros_like(gacc)
        tacc[...] = jnp.zeros_like(tacc)
    else:
        acc[...] = old[0][...]
        gacc[...] = old[1][...]
        tacc[...] = old[2][...]

    def step(j, carry):
        slot = lax.rem(j, 2)
        at = col(j)
        for c in copies(j, slot):
            c.wait()
        down_copy(0, slot).wait()
        cols = pl.ds(at, tf)
        lg = lg_ref[:, cols]
        lu = lu_ref[:, cols]
        ed = ed_ref[:, cols]
        gate = dot(n2_ref[...], wg[slot]) + dot(mg[...], lg)
        up = dot(n2_ref[...], wu[slot]) + dot(mu[...], lu)
        gact = dnt(ct_ref[...], wd[slot]) + dot(gm[...], ed)
        sig = 1.0 / (1.0 + jnp.exp(-gate))
        silu = gate * sig
        act = (silu * up).astype(BF16)
        ggate = (gact * up * sig * (1.0 + gate * (1.0 - sig))).astype(BF16)
        gup = (gact * silu).astype(BF16)
        acc[...] += dot(act, wd[slot])
        gacc[...] += dnt(ggate, wg[slot]) + dnt(gup, wu[slot])
        tacc[0] += dnt(ed, act)
        tacc[1] += dnt(lg, ggate)
        tacc[2] += dnt(lu, gup)
        dlg_ref[:, cols] = dot(mgt[...], ggate).astype(BF16)
        dlu_ref[:, cols] = dot(mut[...], gup).astype(BF16)
        ded_ref[:, cols] = dot(gmt[...], act).astype(BF16)

        @pl.when(j + 2 < nt)
        def _():
            start(j + 2, slot)

        return carry

    lax.fori_loop(0, nt, step, 0)
    if not last:
        return
    zrow = jnp.zeros((128 - RANK, D), BF16)
    md = tacc[0]
    acc[...] += dot(wide(md), jnp.concatenate([ld_ref[...], zrow], axis=0))
    dld_ref[...] = dot(md.astype(BF16), ct_ref[...]).astype(BF16)
    for i in range(2):
        g = tacc[1 + i]
        e = e_ref[i * RANK : (i + 1) * RANK]
        gacc[...] += dot(wide(g), jnp.concatenate([e, zrow], axis=0))
        deg_ref[i * RANK : (i + 1) * RANK] = dot(g.astype(BF16), n2_ref[...]).astype(BF16)
    own_ref[...] = acc[:rows]
    oth_ref[...] = acc[rows:].astype(BF16)
    gown_ref[...] = gacc[:rows]
    goth_ref[...] = gacc[rows:].astype(BF16)


def mlp(pieces, tiles, tf, width, old, last, offs, pos, base, n2, ct, e, ed, lg, lu, ld, arrs, downs):
    m = n2.shape[0]
    rows = m // 2
    first = old is None
    old = [] if first else list(old)
    sums = [((m, D), F32), ((m, D), F32), ((3, RANK, m), F32)]
    slices = tuple(sds((RANK, width), BF16) for _ in range(3))
    if last:
        outs = (
            sds((rows, D), F32),
            sds((rows, D), BF16),
            sds((rows, D), F32),
            sds((rows, D), BF16),
            *slices,
            sds((RANK, D), BF16),
            sds((2 * RANK, D), BF16),
        )
        scratch = [pltpu.VMEM(s, d) for s, d in sums]
    else:
        outs = (*[sds(s, d) for s, d in sums], *slices)
        scratch = []
    return call(
        functools.partial(mlp_body, pieces, tiles, len(arrs), len(downs), tf, width, first, last),
        "mlp",
        outs,
        [offs, pos, base, n2, ct, e, ed, lg, lu, ld, *arrs, *downs, *old],
        [SMEM] * 3 + [VM] * 7 + [ANY] * (len(arrs) + len(downs)) + [VM] * len(old),
        scratch
        + [
            pltpu.VMEM((2, D, tf), BF16),
            pltpu.VMEM((2, D, tf), BF16),
            pltpu.VMEM((2, tf, D), BF16),
            pltpu.VMEM((m, RANK), BF16),
            pltpu.VMEM((m, RANK), BF16),
            pltpu.VMEM((RANK, m), BF16),
            pltpu.VMEM((RANK, m), BF16),
            pltpu.VMEM((m, RANK), BF16),
            pltpu.VMEM((RANK, m), BF16),
            pltpu.SemaphoreType.DMA((2, 2, len(pieces))),
            pltpu.SemaphoreType.DMA((2,)),
        ],
        12 * m * D * width,
        6 * D * width,
    )


def out_back_body(pieces, na, *refs):
    offs, gn_ref, gx_ref, ct_ref, h_ref, g_ref, o_ref, ot_ref, l_ref, mt_ref, lo_ref, et_ref = refs[:12]
    arrs = refs[12 : 12 + na]
    gh_ref, gw_ref, dl_ref, dlo_ref, deo_ref, buf, sem = refs[12 + na :]
    rows = h_ref.shape[0]
    copies = [
        pltpu.make_async_copy(
            arrs[a].at[pl.ds(src, n)], buf.at[pl.ds(pl.multiple_of(offs[i], 16), n)], sem.at[i]
        )
        for i, (a, src, n) in enumerate(pieces)
    ]
    for c in copies:
        c.start()
    h = h_ref[...]
    r = lax.rsqrt(jnp.mean(h * h, axis=-1, keepdims=True) + EPS)
    sc = (gn_ref[...] + gx_ref[...].astype(F32)) * g_ref[...]
    gh = ct_ref[...].astype(F32) + r * sc - h * (r * r * r) * jnp.mean(sc * h, axis=-1, keepdims=True)
    gh_ref[...] = gh
    gb = gh.astype(BF16)
    gmt = dnt(lo_ref[...], gb).astype(BF16)
    dlo_ref[...] = dot(mt_ref[...], gb)
    deo_ref[...] = dot(gmt, o_ref[...])
    for c in copies:
        c.wait()

    def pair(c, carry):
        at = pl.multiple_of(c * 2 * HEAD_DIM, 64)
        g = dnt(buf[pl.ds(at, 2 * HEAD_DIM)], gb) + dot(et_ref[pl.ds(at, 2 * HEAD_DIM)], gmt)
        ot = ot_ref[pl.ds(at, 2 * HEAD_DIM)]
        for i in range(2):
            gi = g[i * HEAD_DIM : (i + 1) * HEAD_DIM]
            inv = 1.0 / l_ref[c][:, i * rows : (i + 1) * rows]
            gw_ref[pl.ds(at + i * HEAD_DIM, HEAD_DIM)] = (gi * inv).astype(BF16)
            d = jnp.sum(gi * ot[i * HEAD_DIM : (i + 1) * HEAD_DIM], axis=0, keepdims=True) * inv
            dl_ref[c, :, i * rows : (i + 1) * rows] = d
        return carry

    lax.fori_loop(0, KV_HEADS, pair, 0)


def out_backward(pieces, offs, gn, gx, ct, h, gain, o_low, ot, ls, mt, lo, et, arrs):
    rows = h.shape[0]
    return call(
        functools.partial(out_back_body, pieces, len(arrs)),
        "out_bwd",
        (
            sds((rows, D), F32),
            sds((D, rows), BF16),
            sds((KV_HEADS, 1, 2 * rows), F32),
            sds((RANK, D), F32),
            sds((RANK, D), F32),
        ),
        [offs, gn, gx, ct, h, gain, o_low, ot, ls, mt, lo, et, *arrs],
        [SMEM] + [VM] * 11 + [ANY] * len(arrs),
        [pltpu.VMEM((D, D), BF16), pltpu.SemaphoreType.DMA((len(pieces),))],
        2 * rows * D * D,
        2 * D * D,
    )


def back_tiles(lo, hi, grad, pieces, arrs, offs, cos_ref, sin_ref, m1t_ref, l_ref, dl_ref, gm, acc, buf, sem):
    def copies(j, slot):
        return column_copies(pieces, arrs, offs, buf, sem, slot, pl.multiple_of(j * TILE, 128), TILE)

    def step(i, carry):
        j = lo + i
        slot = lax.rem(i, 2)
        isv = j >= (D + KVW) // TILE
        blk = jnp.where(j < D // TILE, 0, jnp.where(isv, 2, 1))
        at = pl.multiple_of(i * TILE, 128)
        cos = jnp.where(isv, 1.0, cos_ref[...])
        sin = jnp.where(isv, 0.0, sin_ref[...])
        g = rot_pairs(grad(at), cos, sin, TILE // HEAD_DIM, True).astype(BF16)
        row = pl.ds(pl.multiple_of(blk * RANK, 16), RANK)
        dl_ref[:, pl.ds(at, TILE)] = dnt(m1t_ref[row], g)
        gm[row] += dot(l_ref[:, pl.ds(pl.multiple_of(j * TILE, 128), TILE)], g)
        for c in copies(j, slot):
            c.wait()
        acc[...] += dot(buf[slot], g)

        @pl.when(j + 2 < hi)
        def _():
            for c in copies(j + 2, slot):
                c.start()

        return carry

    for j in range(2):
        for c in copies(lo + j, j):
            c.start()
    lax.fori_loop(0, hi - lo, step, 0)


def q_back_body(pieces, na, *refs):
    offs, gq_ref, cos_ref, sin_ref, m1t_ref, n1_ref, l_ref, et_ref = refs[:8]
    arrs = refs[8 : 8 + na]
    acc, dl_ref, de_ref, buf, gm, sem = refs[8 + na :]
    acc[...] = jnp.zeros_like(acc)
    gm[...] = jnp.zeros_like(gm)
    back_tiles(
        0,
        D // TILE,
        lambda at: gq_ref[pl.ds(at, TILE)],
        pieces, arrs, offs, cos_ref, sin_ref, m1t_ref, l_ref, dl_ref, gm, acc, buf, sem,
    )
    gmb = gm[...].astype(BF16)
    de_ref[...] = dot(gmb[:RANK], n1_ref[...])
    acc[...] += dot(et_ref[...], gmb)


def kv_back_body(pieces, na, nx, *refs):
    offs, gkv_ref = refs[:2]
    rxs = refs[2 : 2 + nx]
    cos_ref, sin_ref, m1t_ref, n1_ref, x_ref, g_ref, gh_ref, l_ref, et_ref, old_ref = refs[2 + nx : 12 + nx]
    arrs = refs[12 + nx : 12 + nx + na]
    gt_ref, dl_ref, de_ref, buf, acc, gm, sem = refs[12 + nx + na :]
    acc[...] = old_ref[...]
    gm[...] = jnp.zeros_like(gm)

    def grad(at):
        g = gkv_ref[pl.ds(at, TILE)]
        for rx in rxs:
            g = g + rx[pl.ds(at, TILE)].astype(F32)
        return g

    back_tiles(
        D // TILE,
        QKV // TILE,
        grad,
        pieces, arrs, offs, cos_ref, sin_ref, m1t_ref, l_ref, dl_ref, gm, acc, buf, sem,
    )
    gmb = gm[...].astype(BF16)
    de_ref[...] = dot(gmb[RANK:], n1_ref[...])
    acc[...] += dot(et_ref[...], gmb)
    x = x_ref[...].astype(F32)
    r = lax.rsqrt(jnp.mean(x * x, axis=-1, keepdims=True) + EPS)
    sc = acc[...].T * g_ref[...]
    gt_ref[...] = gh_ref[...] + r * sc - x * (r * r * r) * jnp.mean(sc * x, axis=-1, keepdims=True)


def q_backward(pieces, offs, gq, cos, sin, m1t, n1, lcat, et, arrs):
    rows = n1.shape[0]
    return call(
        functools.partial(q_back_body, pieces, len(arrs)),
        "q_bwd",
        (sds((D, rows), F32), sds((RANK, D), F32), sds((RANK, D), F32)),
        [offs, gq, cos, sin, m1t, n1, lcat, et, *arrs],
        [SMEM] + [VM] * 7 + [ANY] * len(arrs),
        [
            pltpu.VMEM((2, D, TILE), BF16),
            pltpu.VMEM((3 * RANK, rows), F32),
            pltpu.SemaphoreType.DMA((2, len(pieces))),
        ],
        2 * rows * D * D,
        2 * D * D,
    )


def kv_backward(pieces, offs, gkv, rxs, cos, sin, m1t, n1, x, gain, gh, lcat, et, old, arrs):
    rows = x.shape[0]
    return call(
        functools.partial(kv_back_body, pieces, len(arrs), len(rxs)),
        "kv_bwd",
        (sds((rows, D), F32), sds((RANK, 2 * KVW), F32), sds((2 * RANK, D), F32)),
        [offs, gkv, *rxs, cos, sin, m1t, n1, x, gain, gh, lcat, et, old, *arrs],
        [SMEM] + [VM] * (11 + len(rxs)) + [ANY] * len(arrs),
        [
            pltpu.VMEM((2, D, TILE), BF16),
            pltpu.VMEM((D, rows), F32),
            pltpu.VMEM((3 * RANK, rows), F32),
            pltpu.SemaphoreType.DMA((2, len(pieces))),
        ],
        2 * rows * D * 2 * KVW,
        2 * D * 2 * KVW,
    )


def split_flat(flat, shapes):
    out = []
    at = 0
    for a, b in shapes:
        out.append(flat[at : at + a * b].reshape(a, b))
        at += a * b
    return out


A_SHAPES = [(3 * RANK, D), (RANK, D), (2 * RANK, D), (RANK, FF)]
B_SHAPES = [(RANK, D), (RANK, KVW), (RANK, KVW), (RANK, D), (RANK, FF), (RANK, FF), (RANK, D)]


def shards(ns, nr, tokens, cotangent, segment_ids, adapter_ids, gain1, w_qkv, w_out, gain2, w_gu, w_down, table_a, table_b):
    assert tokens.shape[0] == 1
    x = tokens[0]
    ct = cotangent[0]
    seg = segment_ids[0]
    rows = x.shape[0]
    length = seg.shape[0]
    s = lax.axis_index("shard")
    r = lax.axis_index("rep")
    group = ns // 2
    width = FF // ns
    scope = jax.named_scope

    def over(v, k, name):
        with scope(name):
            return lax.ppermute(v, "shard", [(i, i ^ k) for i in range(ns)])

    def swap(v, k, name):
        with scope(name):
            return lax.ppermute(v, "rep", [(i, i ^ k) for i in range(nr)])

    def shift(v, k, name):
        with scope(name):
            return lax.ppermute(v, "shard", [(i, i + k) for i in range(ns) if 0 <= i + k < ns])

    every = list(range(1, ns))
    near = list(range(1, group))

    a = adapter_ids[0]
    row_a = lax.dynamic_slice_in_dim(table_a, a, 1, 0)
    row_b = lax.dynamic_slice_in_dim(table_b, a, 1, 0)
    na, nb = row_a.shape[1], row_b.shape[1]
    line = jnp.concatenate([row_a, row_b], axis=1)
    lines = [line] + [over(line, k, f"t_ad_{k}") for k in every]
    both = jnp.zeros((ns, na + nb), BF16)
    for k, v in enumerate(lines):
        both = lax.dynamic_update_slice_in_dim(both, v, s ^ k, 0)
    e_qkv, e_out, e_gu, e_down = split_flat(both[:, :na].reshape(-1), A_SHAPES)
    l_q, l_k, l_v, l_out, l_gate, l_up, l_down = split_flat(both[:, na:].reshape(-1), B_SHAPES)
    lcat = jnp.concatenate([l_q, l_k, l_v], axis=1)

    def gather(own, ks, send, name, parts, unit=16):
        n = own.shape[0]
        if n % (unit * parts) or nr % parts:
            parts = 1
        q = n // parts
        me = r & (parts - 1)
        got = [over(send(k, me * q, q), k, f"t_{name}_{k}") for k in ks]
        arrs, pieces = [own], [(0, 0, n)]
        kv, fv = [0], [-1]

        def add(v, k, flip, src):
            pieces.append((len(arrs) - 1, src, q))
            kv.append(k)
            fv.append(flip)

        for k, v in zip(ks, got):
            arrs.append(v)
            add(v, k, 0, 0)
            if parts > 1:
                arrs.append(swap(v, 1, f"c_{name}_{k}"))
                add(v, k, 1, 0)
        if parts == 4:
            cat = jnp.concatenate(got, axis=0) if len(ks) > 1 else got[0]
            far = swap(cat, 2, f"z_{name}")
            for flip, v in ((2, far), (3, swap(far, 1, f"d_{name}"))):
                arrs.append(v)
                for i, k in enumerate(ks):
                    add(v, k, flip, i * q)
        kv, fv = np.array(kv, np.int32), np.array(fv, np.int32)
        part = jnp.where(fv < 0, 0, me ^ jnp.maximum(fv, 0))
        return arrs, pieces, (s ^ kv), part, q

    def row_gather(own, name, parts):
        arrs, pieces, sh, part, q = gather(
            own, every, lambda k, at, n: lax.dynamic_slice_in_dim(own, at, n, 0), name, parts
        )
        return arrs, pieces, (sh * own.shape[0] + part * q).astype(jnp.int32)

    qkv_arrs, qkv_pieces, qkv_offs = row_gather(w_qkv, "qkv", 2)
    out_arrs, out_pieces, out_offs = row_gather(w_out, "out", 4)
    tf = min(256, width)
    blocks = []
    for m in range(group):

        def cols(k, at, n, m=m):
            c = (s ^ k ^ m) * width
            return jnp.concatenate(
                [
                    lax.dynamic_slice(w_gu, (at, c), (n, width)),
                    lax.dynamic_slice(w_gu, (at, FF + c), (n, width)),
                ],
                axis=1,
            )

        arrs, pieces, sh, part, q = gather(w_gu, every, cols, f"gu{m}", 4)
        offs = (sh * w_gu.shape[0] + part * q).astype(jnp.int32)
        if m == 0:
            downs, dp, dpart, dq = [w_down], [(0, 0, w_down.shape[0])], np.zeros(1, np.int32), 0
        else:
            downs, dp, _, dpart, dq = gather(
                w_down,
                [m],
                lambda k, at, n: lax.dynamic_slice_in_dim(w_down, at, n, 0),
                f"down{m}",
                4,
                tf,
            )
            downs, dp, dpart = downs[1:], [(i - 1, src, n) for i, src, n in dp[1:]], dpart[1:]
        tiles, of, add = [], [], []
        for i, (ai, src, n) in enumerate(dp):
            for u in range(n // tf):
                tiles.append((ai, src + u * tf))
                of.append(i)
                add.append(u)
        pos = (dpart * dq // tf)[np.array(of)] + np.array(add, np.int32)
        at = (s ^ m) * width
        blocks.append((arrs, pieces, offs, downs, tiles, jnp.asarray(pos, jnp.int32), at))

    positions = s * rows + jnp.arange(rows, dtype=jnp.int32)
    freq = ROPE_BASE ** (-(jnp.arange(HALF, dtype=F32) * 2.0 / HEAD_DIM))
    angles = freq[:, None] * positions.astype(F32)[None, :]
    cos, sin = jnp.cos(angles), jnp.sin(angles)

    halo = min(ns - 1, -(-(length // 2 - 1) // rows))
    base = (s * rows).reshape(1).astype(jnp.int32)
    qseg = lax.dynamic_slice_in_dim(seg, s * rows, rows, 0)[None, :]
    kseg = jnp.concatenate(
        [
            lax.dynamic_slice_in_dim(seg, jnp.maximum(s - b, 0) * rows, rows, 0)
            for b in range(halo + 1)
        ]
    )[:, None]
    g1 = gain1[None, :]
    g2 = gain2[None, :]

    ct_both = jnp.concatenate([ct, over(ct, group, "t_ct")], axis=0)
    kvt, n1, m1t, mid = kv_forward(qkv_pieces, qkv_offs, x, g1, e_qkv, lcat, cos, sin, qkv_arrs)
    kvs = [kvt] + [shift(kvt, b, f"t_kv_{b}") for b in range(1, halo + 1)]
    qt = q_forward(qkv_pieces, qkv_offs, n1, mid, lcat, cos, sin, qkv_arrs)
    ot, ls, o_low = attention_forward(base, qseg, kseg, qt, kvs)
    hidden, n2, mt = out_forward(out_pieces, out_offs, o_low, x, g2, e_out, l_out, out_arrs)
    n2_both = jnp.concatenate([n2, over(n2, group, "t_n2")], axis=0)

    wide_grads = [jnp.zeros((RANK, FF), BF16) for _ in range(3)]
    old = None
    for m, (arrs, pieces, offs, downs, tiles, pos, at) in enumerate(blocks):

        def part_of(v, at=at):
            return lax.dynamic_slice_in_dim(v, at, width, 1)

        last = m == len(blocks) - 1
        res = mlp(
            pieces, tiles, tf, width, old, last, offs, pos, at.reshape(1).astype(jnp.int32),
            n2_both, ct_both, e_gu, part_of(e_down), part_of(l_gate), part_of(l_up), l_down, arrs, downs,
        )
        if last:
            own, oth, gown, goth = res[:4]
            dld, deg = res[7:]
            three = res[4:7]
        else:
            old, three = res[:3], res[3:]
        wide_grads = [
            lax.dynamic_update_slice_in_dim(w, v, at, 1) for w, v in zip(wide_grads, three)
        ]
    dlg, dlu, ded = wide_grads
    gx = over(goth, group, "t_gn2")
    output = (hidden + own + over(oth, group, "t_out").astype(F32)).astype(BF16)
    gh, gw, delta, dlo, deo = out_backward(
        out_pieces, out_offs, gown, gx, ct, hidden, g2, o_low, ot, ls, mt, l_out, e_out.T, out_arrs
    )
    gq = None
    rxs = []
    if halo:
        far = list(range(1, halo + 1))
        gq, *gfar = attention_backward(
            far, base, qseg, kseg[rows:], qt, gw, delta, kvs[1:], None, BF16
        )
        rxs = [shift(g, -b, f"t_dkv_{b}") for b, g in zip(far, gfar)]
    gq, gkv = attention_backward([0], base, qseg, kseg[:rows], qt, gw, delta, kvs[:1], gq, F32)
    et = e_qkv.T
    part_n1, dlq, deq_q = q_backward(qkv_pieces, qkv_offs, gq, cos, sin, m1t, n1, lcat, et, qkv_arrs)
    grad_tokens, dlkv, deq_kv = kv_backward(
        qkv_pieces, qkv_offs, gkv, rxs, cos, sin, m1t, n1, x, g1, gh, lcat, et, part_n1, qkv_arrs
    )

    def flat(parts):
        return jnp.concatenate([v.astype(BF16).reshape(-1) for v in parts]).reshape(ns, -1)

    ga = flat([deq_q, deq_kv, deo, deg, ded])
    gb = flat([dlq, dlkv[:, :KVW], dlkv[:, KVW:], dlo, dlg, dlu, dld])
    send = jnp.concatenate([ga, gb], axis=1)

    def chunk(k):
        return lax.dynamic_slice_in_dim(send, s ^ k, 1, 0)

    mine = chunk(0).astype(F32)
    for k in every:
        mine = mine + over(chunk(k), k, f"t_ga_{k}").astype(F32)
    hot = (a == jnp.arange(128)).astype(BF16)[None]
    mine = mine.astype(BF16)
    hw = (na + nb) // 2
    c = r & 1

    def half_of(v, c):
        return lax.dynamic_slice_in_dim(v, c * hw, hw, 1)

    there = swap(jnp.concatenate([half_of(mine, 1 - c), hot], axis=1), 1, "c_ga")
    here = jnp.concatenate([jnp.concatenate([half_of(mine, c), hot], axis=1), there], axis=0)
    lines = jnp.zeros((nr, hw + 128), BF16)
    for k in range(0, nr, 2):
        v = swap(here, k, f"z_ga_{k}") if k else here
        lines = lax.dynamic_update_slice_in_dim(lines, v, (r ^ k) & ~1, 0)
    total = lax.dot_general(
        lines[:, hw : hw + ADAPTERS], lines[:, :hw], (((0,), (0,)), ((), ())), preferred_element_type=F32
    )
    total = total.astype(BF16)
    other = swap(total, 1, "c_tot")
    total = jnp.concatenate(
        [jnp.where(c == 0, total, other), jnp.where(c == 0, other, total)], axis=1
    ).astype(F32)
    return output[None], grad_tokens[None], total[:, :na], total[:, na:]


def solution(mesh):
    ns, nr = mesh.shape["shard"], mesh.shape["rep"]
    seqs = P("rep", "shard", None)
    frozen = P("shard", None)
    tables = P(None, "shard")
    return jax.shard_map(
        functools.partial(shards, ns, nr),
        mesh=mesh,
        in_specs=(seqs, seqs, P("rep", None), P("rep"), P(), frozen, frozen, P(), frozen, frozen, tables, tables),
        out_specs=(seqs, seqs, tables, tables),
        check_vma=False,
    )
```
